32 devices in a mesh: section: 4 (over y, core), tok: 8 (over z, x).
Axes of the slice: x: 2, y: 2, z: 4, core: 2. Of those that a mesh axis runs over, the one named last changes fastest.
Arguments:
- patches: bfloat16 [1024, 6144], P('tok'), may hold values from -6 to 6
- patch_ids: int32 [1024], P('tok'), may hold values from 0 to 255
- pos_table: bfloat16 [256, 6144], replicated, may hold values from -5 to 5
- token_counts: int32 [8], P('tok'), may hold values from 16 to 128, as said below
- norm_gain: float32 [4, 6144], P('section'), may hold values from 0.25 to 1.75
- norm_bias: float32 [4, 6144], P('section'), may hold values from -3 to 3
- branch_scale: float32 [4, 6144], P('section'), may hold values from 0.5 to 2
- act_range: float32 [4, 6144], P('section'), may hold values from 1 to 8
- weight_range: float32 [4, 6144], P('section'), may hold values from 0.125 to 1
- alpha_index: int32 [4], P('section'), may hold values from 2 to 7
Outputs:
- covariance: float32 [4, 128, 6144], P('section')
- channel_mean: float32 [4, 6144], P('section')
The draws below stay inside these ranges and needn't reach their ends.
Inputs may be any that keep to these rules, and one draw needn't show every extreme that they name: Each shard's calibration tokens are its first token_counts slots; at least one shard is full in every draw.
All inputs are finite; a program needn't handle non-finite values.
Results may differ from the reference program's by a relative error of at most 0.0067.
Values may be sent and summed in bfloat16 or wider, within the bound.
No kernel may reach another device: no remote copies, remote signals or barrier semaphores. Data moves between devices by JAX's collectives and lax.ppermute only.
A program may use at most 256 MiB of HBM per device.

```python
import math
import jax
import jax.numpy as jnp
from jax import lax

D = 6144
BLOCK = 128
PATCHES = 256
TOK_DEV = 128
TOKENS = 1024
LAYERS = 4
N_TOK = 8


def draw_token_counts(key, part):
    drawn = jax.random.randint(key, (N_TOK,), TOK_DEV // 8, TOK_DEV + 1)
    full_shard = jax.random.randint(jax.random.fold_in(key, 7), (), 0, N_TOK)
    shard_ids = jnp.arange(N_TOK, dtype=jnp.int32)
    return jnp.where(shard_ids == full_shard, TOK_DEV, drawn).astype(jnp.int32)


def place_ends(array, rng, least, largest):
    extent = array.shape
    place = [jax.random.randint(jax.random.fold_in(rng, axis), (), 0, extent[axis]) for axis in range(len(extent))]
    array = array.at[tuple(place)].set(least)
    longest = extent.index(max(extent))
    place[longest] = (place[longest] + 1) % extent[longest]
    return array.at[tuple(place)].set(largest)


def block_scale(key, extent, split, least, top_value):
    level = 1.0
    for position, parts in split:
        draws = jax.random.uniform(jax.random.fold_in(jax.random.fold_in(key, 6), position), (parts,), jnp.float32, least / len(split), top_value / len(split))
        level = level * jnp.repeat(jnp.exp(draws), extent[position] // parts).reshape((-1,) + (1,) * (len(extent) - 1 - position))
    return level


def bell_draw(rng, shape, scale, reach, cuts=(), kind=jnp.bfloat16):
    entries = scale * jax.random.normal(rng, shape, jnp.float32)
    if cuts:
        entries = entries * block_scale(rng, shape, cuts, -0.22, 0.18)
    return jnp.clip(entries, -reach, reach).astype(kind)


def setup_inputs(seed: int = 0) -> dict:
    key_list = jax.random.split(jax.random.key(seed), 11)
    return {
        "patches": bell_draw(key_list[0], (TOKENS, D), 1.0, 6.0, ((0, 8),)),
        "patch_ids": place_ends(jax.random.randint(key_list[1], (TOKENS,), 0, PATCHES), jax.random.fold_in(key_list[1], 1), 0, PATCHES - 1).astype(jnp.int32),
        "pos_table": bell_draw(key_list[2], (PATCHES, D), 0.7, 5.0),
        "token_counts": draw_token_counts(jax.random.fold_in(key_list[10], 71), 0),
        "norm_gain": jnp.clip(1.0 + 0.15 * jax.random.normal(key_list[4], (LAYERS, D), jnp.float32), 0.25, 1.75),
        "norm_bias": bell_draw(key_list[5], (LAYERS, D), 0.5, 3.0, ((0, 4),), jnp.float32),
        "branch_scale": jnp.clip(0.5 + 1.5 * jax.random.uniform(key_list[6], (LAYERS, D), jnp.float32) ** block_scale(key_list[6], (LAYERS, D), ((0, 4),), -0.2, 0.2), 0.5, 2.0),
        "act_range": jnp.clip(jnp.exp(math.log(8.0) - 2.0794415 * jax.random.uniform(key_list[7], (LAYERS, D), jnp.float32) ** block_scale(key_list[7], (LAYERS, D), ((0, 4),), -0.2, 0.2)), 1.0, 8.0),
        "weight_range": jnp.clip(jnp.exp(math.log(1.0) - 2.0794415 * jax.random.uniform(key_list[8], (LAYERS, D), jnp.float32) ** block_scale(key_list[8], (LAYERS, D), ((0, 4),), -0.2, 0.2)), 0.125, 1.0),
        "alpha_index": place_ends(jax.random.randint(key_list[9], (LAYERS,), 2, 8), jax.random.fold_in(key_list[9], 1), 2, 7).astype(jnp.int32),
    }


def layer_norm(values, gain, bias_row):
    centre = lax.optimization_barrier(jnp.mean(values, axis=-1, keepdims=True))
    spread = lax.optimization_barrier(jnp.mean(jnp.square(values - centre), axis=-1, keepdims=True))
    return (values - centre) * lax.rsqrt(spread + 1e-06) * gain + bias_row

def smoothing(act_row, weight_row, alpha_code):
    exponent = alpha_code.astype(jnp.float32) / 8.0
    return jnp.exp(exponent * jnp.log(act_row) + (exponent - 1.0) * jnp.log(weight_row))

def reference(patches, patch_ids, pos_table, token_counts, norm_gain, norm_bias, branch_scale, act_range, weight_range, alpha_index):
    looked_up = jnp.take(pos_table, patch_ids, axis=0).astype(jnp.float32)
    hidden = (patches.astype(jnp.float32) + looked_up).astype(jnp.bfloat16)
    positions = jnp.arange(TOK_DEV, dtype=jnp.int32)
    valid_rows = (positions[None, :] < token_counts[:, None]).reshape(TOKENS).astype(jnp.float32)
    tokens_used = jnp.sum(valid_rows)
    cov_list = []
    mean_list = []
    for layer_idx in range(LAYERS):
        normed = layer_norm(hidden.astype(jnp.float32), norm_gain[layer_idx], norm_bias[layer_idx])
        factor = smoothing(act_range[layer_idx], weight_range[layer_idx], alpha_index[layer_idx])
        smoothed = (normed / factor).astype(jnp.bfloat16)
        weighted = smoothed.astype(jnp.float32) * valid_rows[:, None]
        mean_row = lax.optimization_barrier(jnp.sum(weighted, axis=0)) / tokens_used
        centred = (smoothed.astype(jnp.float32) - mean_row[None, :]) * valid_rows[:, None]
        gram_block = jnp.dot(centred[:, :BLOCK].T, centred, precision=lax.Precision.HIGHEST, preferred_element_type=jnp.float32)
        cov_list.append(gram_block / tokens_used)
        mean_list.append(mean_row)
        hidden = (hidden.astype(jnp.float32) + branch_scale[layer_idx] * jax.nn.gelu(normed)).astype(jnp.bfloat16)
    return (jnp.stack(cov_list), jnp.stack(mean_list))
```

```python
import functools

import jax
import jax.numpy as jnp
from jax import lax
from jax.experimental import pallas as pl
from jax.experimental.pallas import tpu as pltpu
from jax.sharding import PartitionSpec as P

LANES = 128
CORES = 2
PARTS = 3
PARAM_ROWS = 4
EXTRA_ROWS = 8
EPS = 1e-06
GELU_A = 0.7978845608028654
GELU_B = 0.044715 * GELU_A
VMEM = pl.BlockSpec(memory_space=pltpu.VMEM)
SMEM = pl.BlockSpec(memory_space=pltpu.SMEM)

BLOCK = 128
MICRO = 4


def from_behind(block, axis, distance):
    devices = range(lax.axis_size(axis))
    route = [(i - distance, i) for i in devices if i - distance in devices]
    return lax.ppermute(block, axis, route)


def layer_norm(values, gain, bias_row):
    centre = jnp.mean(values, axis=-1, keepdims=True)
    spread = jnp.mean(jnp.square(values - centre), axis=-1, keepdims=True)
    return (values - centre) * lax.rsqrt(spread + 1e-06) * gain + bias_row


def smoothing(act_row, weight_row, alpha_code):
    exponent = alpha_code.astype(jnp.float32) / 8.0
    return jnp.exp(exponent * jnp.log(act_row) + (exponent - 1.0) * jnp.log(weight_row))


def about_mean(sum_second, sum_first, own_count, mean_row):
    cross = (
        sum_first[:BLOCK][:, None] * mean_row[None, :]
        + mean_row[:BLOCK][:, None] * sum_first[None, :]
    )
    return sum_second - cross + own_count * (mean_row[:BLOCK][:, None] * mean_row[None, :])


def pipelined_body(
    patches,
    patch_ids,
    pos_table,
    token_counts,
    norm_gain,
    norm_bias,
    branch_scale,
    act_range,
    weight_range,
    alpha_index,
):
    sections = lax.axis_size("section")
    section_index = lax.axis_index("section")
    rows_here = patches.shape[0]
    width = patches.shape[1]
    micro_rows = rows_here // MICRO
    looked_up = jnp.take(pos_table, patch_ids, axis=0).astype(jnp.float32)
    start_rows = (patches.astype(jnp.float32) + looked_up).astype(jnp.bfloat16)
    positions = jnp.arange(rows_here, dtype=jnp.int32)
    valid_flat = (positions < token_counts[0]).astype(jnp.float32)
    factor = smoothing(act_range[0], weight_range[0], alpha_index[0])
    blocks = start_rows.reshape(MICRO, micro_rows, width)
    valid_rows = valid_flat.reshape(MICRO, micro_rows)

    def tick_step(tick, carry):
        incoming, stash = carry
        micro_index = tick - section_index
        active = jnp.logical_and(micro_index >= 0, micro_index < MICRO)
        safe_index = jnp.clip(micro_index, 0, MICRO - 1)
        own_block = lax.dynamic_index_in_dim(blocks, safe_index, 0, keepdims=False)
        current = jnp.where(section_index == 0, own_block, incoming)
        normed = layer_norm(current.astype(jnp.float32), norm_gain[0], norm_bias[0])
        smoothed = (normed / factor).astype(jnp.bfloat16)
        weight_mask = lax.dynamic_index_in_dim(valid_rows, safe_index, 0, keepdims=False).astype(
            jnp.bfloat16
        )
        masked = smoothed * weight_mask[:, None]
        previous = lax.dynamic_index_in_dim(stash, safe_index, 0, keepdims=False)
        kept = jnp.where(active, masked, previous)
        stash = lax.dynamic_update_index_in_dim(stash, kept, safe_index, 0)
        updated = (current.astype(jnp.float32) + branch_scale[0] * jax.nn.gelu(normed)).astype(
            jnp.bfloat16
        )
        passed = from_behind(updated, "section", 1)
        return (passed, stash)

    initial = (
        jnp.zeros((micro_rows, width), jnp.bfloat16),
        jnp.zeros((MICRO, micro_rows, width), jnp.bfloat16),
    )
    carried = lax.fori_loop(0, sections + MICRO - 1, tick_step, initial)
    masked = carried[1].reshape(rows_here, width)
    ones_row = jnp.ones((1, rows_here), jnp.bfloat16)
    sum_first = jnp.dot(ones_row, masked, preferred_element_type=jnp.float32)[0]
    sum_second = lax.dot_general(
        masked[:, :BLOCK], masked, (((0,), (0,)), ((), ())), preferred_element_type=jnp.float32
    )
    own_count = token_counts.astype(jnp.float32)
    total_count, channel_sums = lax.psum((own_count, sum_first), "tok")
    mean_row = channel_sums / total_count
    gram_block = lax.psum(about_mean(sum_second, sum_first, own_count, mean_row), "tok")
    return ((gram_block / total_count)[None], mean_row[None])


def swap(block, axis, mask):
    route = [(i, i ^ mask) for i in range(lax.axis_size(axis))]
    return lax.ppermute(block, axis, route)


def split_parts(value):
    parts = []
    for _ in range(PARTS):
        part = value.astype(jnp.bfloat16).astype(jnp.float32)
        parts.append(part)
        value = value - part
    return parts


def gelu_update(x, normed, scale):
    inner = normed * (GELU_A + GELU_B * (normed * normed))
    return x + (0.5 * scale) * (normed * (1.0 + jnp.tanh(inner)))


def params_kernel(gain, bias, scale, act, weight, alpha, out):
    exponent = alpha[0].astype(jnp.float32) / 8.0
    out[0:1, :] = gain[...]
    out[1:2, :] = bias[...]
    out[2:3, :] = scale[...]
    out[3:4, :] = jnp.exp((1.0 - exponent) * jnp.log(weight[...]) - exponent * jnp.log(act[...]))


def embed_kernel(patches, ids, table, out, onehot):
    rows, half = patches.shape[0], out.shape[0]
    core = lax.rem(lax.axis_index("section"), CORES)
    positions = table.shape[0]

    @pl.when(pl.program_id(0) == 0)
    def _():
        hits = lax.broadcasted_iota(jnp.int32, (positions, rows), 0) == ids[...]
        onehot[...] = jnp.transpose(hits.astype(jnp.float32)).astype(jnp.bfloat16)

    mine = pl.ds(pl.multiple_of(core * half, half), half)
    looked_up = jnp.dot(onehot[mine, :], table[...], preferred_element_type=jnp.float32)
    out[...] = (patches[mine, :].astype(jnp.float32) + looked_up).astype(jnp.bfloat16)


def stats_kernel(n_sec, n_tok, width, rb, *refs):
    hid, counts = refs[0], refs[1]
    tables = refs[2 : 2 + n_sec]
    outs = refs[2 + n_sec : 2 + n_sec + n_tok]
    par, state, tile = refs[2 + n_sec + n_tok :]
    half, depth = hid.shape
    columns = depth // LANES
    sec, tok = lax.axis_index("section"), lax.axis_index("tok")
    core, group = lax.rem(sec, CORES), lax.div(sec, CORES)
    groups = n_sec // CORES
    for k in range(n_sec):
        par[jnp.bitwise_xor(sec, k)] = tables[k][...]
    lane = lax.broadcasted_iota(jnp.int32, (rb, LANES), 1)

    def total(terms):
        acc = [None] * 4
        for i, term in enumerate(terms):
            acc[i % 4] = term if acc[i % 4] is None else acc[i % 4] + term
        return jnp.sum((acc[0] + acc[1]) + (acc[2] + acc[3]), axis=-1, keepdims=True)

    def col(c):
        return slice(c * LANES, (c + 1) * LANES)

    def measure_rows(layer):
        mu = total(state[:, col(c)].astype(jnp.float32) for c in range(columns)) * (1.0 / depth)
        var = total(
            jnp.square(state[:, col(c)].astype(jnp.float32) - mu) for c in range(columns)
        ) * (1.0 / depth)
        rstd = lax.rsqrt(var + EPS)
        found = tile[...]
        for v, value in enumerate((mu, rstd)):
            for p, part in enumerate(split_parts(value)):
                found = jnp.where(lane == (2 * layer + v) * PARTS + p, part, found)
        tile[...] = found
        return mu, rstd

    @pl.loop(0, half // rb)
    def _(block):
        rows = pl.ds(pl.multiple_of(block * rb, rb), rb)
        row_id = lax.broadcasted_iota(jnp.int32, (rb, LANES), 0) + core * half + block * rb
        valid = (row_id < counts[0]).astype(jnp.float32)
        tile[...] = jnp.where(lane == 2 * n_sec * PARTS, valid, 0.0)
        state[...] = hid[rows, :]

        @pl.loop(0, n_sec - 1)
        def _(layer):
            mu, rstd = measure_rows(layer)
            for c in range(columns):
                x = state[:, col(c)].astype(jnp.float32)
                normed = (x - mu) * rstd * par[layer, 0:1, col(c)] + par[layer, 1:2, col(c)]
                state[:, col(c)] = gelu_update(x, normed, par[layer, 2:3, col(c)]).astype(
                    jnp.bfloat16
                )

        measure_rows(n_sec - 1)
        packed = tile[...].astype(jnp.bfloat16)
        for k in range(n_tok):
            peer = jnp.bitwise_xor(tok, k)
            first = pl.multiple_of((peer * groups + group) * width, LANES)
            outs[k][rows, 0:width] = hid[rows, pl.ds(first, width)]
            outs[k][rows, width : width + BLOCK] = hid[rows, 0:BLOCK]
            outs[k][rows, width + BLOCK : width + BLOCK + LANES] = packed


def moments_kernel(n_sec, n_tok, width, *refs):
    messages = refs[:n_tok]
    tables = refs[n_tok : n_tok + n_sec]
    keep, give = refs[n_tok + n_sec : n_tok + n_sec + 2]
    par, msg, sel, dec, smoothed, count = refs[n_tok + n_sec + 2 :]
    half = messages[0].shape[0]
    span = width + BLOCK
    blocks = 2 * n_sec + 1
    sec, tok = lax.axis_index("section"), lax.axis_index("tok")
    core, group = lax.rem(sec, CORES), lax.div(sec, CORES)
    groups = n_sec // CORES
    first = pl.multiple_of((tok * groups + group) * width, LANES)
    for k in range(n_sec):
        layer = jnp.bitwise_xor(sec, k)
        par[layer, :, 0:width] = tables[k][:, pl.ds(first, width)]
        par[layer, :, width:span] = tables[k][:, 0:BLOCK]
    for k in range(n_tok):
        msg[k] = messages[k][...]
    for q in range(blocks):
        row = lax.broadcasted_iota(jnp.int32, (LANES, LANES), 0)
        hit = jnp.logical_and(row >= q * PARTS, row < (q + 1) * PARTS)
        sel[:, q * LANES : (q + 1) * LANES] = hit.astype(jnp.float32).astype(jnp.bfloat16)
    count[...] = jnp.zeros_like(count)

    @pl.loop(0, n_tok)
    def _(k):
        dec[...] = jnp.dot(
            msg[k, :, span : span + LANES], sel[...], preferred_element_type=jnp.float32
        )
        valid = dec[:, 2 * n_sec * LANES : (2 * n_sec + 1) * LANES]
        count[...] += jnp.sum(valid.reshape(half // 8, 8, LANES), axis=0)
        rows = pl.ds(pl.multiple_of(k * half, half), half)
        for c in range(span // LANES):
            cols = slice(c * LANES, (c + 1) * LANES)
            x = msg[k, :, cols].astype(jnp.float32)
            for layer in range(n_sec):
                mu = dec[:, 2 * layer * LANES : (2 * layer + 1) * LANES]
                rstd = dec[:, (2 * layer + 1) * LANES : (2 * layer + 2) * LANES]
                normed = (x - mu) * rstd * par[layer, 0:1, cols] + par[layer, 1:2, cols]
                smoothed[layer, rows, cols] = (normed * par[layer, 3:4, cols] * valid).astype(
                    jnp.bfloat16
                )
                if layer < n_sec - 1:
                    x = gelu_update(x, normed, par[layer, 2:3, cols])
                    x = x.astype(jnp.bfloat16).astype(jnp.float32)

    ones = jnp.ones((8, n_tok * half), jnp.bfloat16)
    used = jnp.sum(count[...], axis=0, keepdims=True)
    for target, parity in ((keep, core), (give, 1 - core)):
        for j in range(groups):
            layer = CORES * j + parity
            values = smoothed[layer]
            lead = values[:, width:span]
            target[j, 0:BLOCK, :] = lax.dot_general(
                lead,
                values[:, 0:width],
                (((0,), (0,)), ((), ())),
                preferred_element_type=jnp.float32,
            )
            sums = jnp.dot(ones, values, preferred_element_type=jnp.float32)
            target[j, BLOCK : BLOCK + EXTRA_ROWS, :] = jnp.zeros((EXTRA_ROWS, width), jnp.float32)
            target[j, BLOCK : BLOCK + 1, :] = sums[0:1, 0:width]
            target[j, BLOCK + 1 : BLOCK + 2, 0:BLOCK] = sums[0:1, width:span]
            target[j, BLOCK + 2 : BLOCK + 3, 0:LANES] = used


def centre_kernel(groups, keep, other, *outs):
    width = keep.shape[2]
    group = lax.div(lax.axis_index("section"), CORES)
    for k in range(groups):
        j = jnp.bitwise_xor(group, k)
        tail = keep[j, BLOCK : BLOCK + EXTRA_ROWS, :] + other[j, BLOCK : BLOCK + EXTRA_ROWS, :]
        inverse = 1.0 / tail[2:3, 0:LANES]
        lead = jnp.broadcast_to(tail[1:2, 0:BLOCK] * inverse, (BLOCK, BLOCK))
        lead = jnp.transpose(lead)
        row_id = lax.broadcasted_iota(jnp.int32, (EXTRA_ROWS, LANES), 0)
        for c in range(width // LANES):
            cols = slice(c * LANES, (c + 1) * LANES)
            mean = tail[0:1, cols] * inverse
            second = keep[j, 0:BLOCK, cols] + other[j, 0:BLOCK, cols]
            outs[k][0:BLOCK, cols] = (second * inverse - lead * mean).astype(jnp.bfloat16)
            extra = jnp.zeros((EXTRA_ROWS, LANES), jnp.float32)
            for p, part in enumerate(split_parts(mean)):
                extra = jnp.where(row_id == p, part, extra)
            outs[k][BLOCK : BLOCK + EXTRA_ROWS, cols] = extra.astype(jnp.bfloat16)


def join_kernel(groups, *refs):
    pieces, out = refs[:groups], refs[groups]
    width = pieces[0].shape[1]
    group = lax.div(lax.axis_index("section"), CORES)
    for k in range(groups):
        first = pl.multiple_of(jnp.bitwise_xor(group, k) * width, LANES)
        out[:, pl.ds(first, width)] = pieces[k][...]


def spread_kernel(n_tok, *refs):
    pieces, cov, mean = refs[:n_tok], refs[n_tok], refs[n_tok + 1]
    width = pieces[0].shape[1]
    tok = lax.axis_index("tok")
    for k in range(n_tok):
        first = pl.multiple_of(jnp.bitwise_xor(tok, k) * width, LANES)
        for c in range(width // LANES):
            cols = slice(c * LANES, (c + 1) * LANES)
            value = pieces[k][:, cols].astype(jnp.float32)
            cov[0, :, pl.ds(first + c * LANES, LANES)] = value[0:BLOCK, :]
            row = value[BLOCK : BLOCK + 1, :]
            for p in range(1, PARTS):
                row = row + value[BLOCK + p : BLOCK + p + 1, :]
            mean[0:1, pl.ds(first + c * LANES, LANES)] = row


def call(kernel, outs, n_in, scratch=(), smem=(), cost=None, name=None):
    return pl.pallas_call(
        kernel,
        out_shape=outs,
        in_specs=[SMEM if i in smem else VMEM for i in range(n_in)],
        out_specs=jax.tree.map(lambda _: VMEM, outs),
        scratch_shapes=list(scratch),
        cost_estimate=cost,
        name=name,
    )


def cost(flops, moved, slow=0):
    return pl.CostEstimate(flops=flops, bytes_accessed=moved, transcendentals=slow)


def sharded_body(
    patches,
    patch_ids,
    pos_table,
    token_counts,
    norm_gain,
    norm_bias,
    branch_scale,
    act_range,
    weight_range,
    alpha_index,
):
    n_sec, n_tok = lax.axis_size("section"), lax.axis_size("tok")
    groups = n_sec // CORES
    rows, depth = patches.shape
    half = rows // CORES
    positions = pos_table.shape[0]
    width = depth // (n_tok * groups)
    span = width + BLOCK
    f32, bf16 = jnp.float32, jnp.bfloat16
    shape = jax.ShapeDtypeStruct

    own = call(params_kernel, shape((PARAM_ROWS, depth), f32), 6, smem=(5,), name="params")(
        norm_gain, norm_bias, branch_scale, act_range, weight_range, alpha_index
    )
    tables = [own] + [swap(own, "section", k) for k in range(1, n_sec)]

    step = depth // n_tok
    hidden = pl.pallas_call(
        embed_kernel,
        out_shape=shape((half, depth), bf16),
        grid=(n_tok,),
        in_specs=[
            pl.BlockSpec((rows, step), lambda i: (0, i)),
            pl.BlockSpec((1, rows), lambda i: (0, 0)),
            pl.BlockSpec((positions, step), lambda i: (0, i)),
        ],
        out_specs=pl.BlockSpec((half, step), lambda i: (0, i)),
        scratch_shapes=[pltpu.VMEM((rows, positions), bf16)],
        cost_estimate=cost(2 * half * positions * depth, 2 * depth * (rows + positions + half)),
        name="embed",
    )(patches, patch_ids.reshape(1, rows), pos_table)

    rb = 32 if half % 32 == 0 else 16
    work = half * depth * n_sec
    message = shape((half, span + LANES), bf16)
    messages = call(
        functools.partial(stats_kernel, n_sec, n_tok, width, rb),
        [message] * n_tok,
        2 + n_sec,
        scratch=[
            pltpu.VMEM((n_sec, PARAM_ROWS, depth), f32),
            pltpu.VMEM((rb, depth), bf16),
            pltpu.VMEM((rb, LANES), f32),
        ],
        smem=(1,),
        cost=cost(20 * work, 2 * half * depth, work),
        name="stats",
    )(hidden, token_counts, *tables)
    messages = [messages[0]] + [swap(messages[k], "tok", k) for k in range(1, n_tok)]

    partial = shape((groups, BLOCK + EXTRA_ROWS, width), f32)
    keep, give = call(
        functools.partial(moments_kernel, n_sec, n_tok, width),
        [partial, partial],
        n_tok + n_sec,
        scratch=[
            pltpu.VMEM((n_sec, PARAM_ROWS, span), f32),
            pltpu.VMEM((n_tok, half, span + LANES), bf16),
            pltpu.VMEM((LANES, (2 * n_sec + 1) * LANES), bf16),
            pltpu.VMEM((half, (2 * n_sec + 1) * LANES), f32),
            pltpu.VMEM((n_sec, n_tok * half, span), bf16),
            pltpu.VMEM((8, LANES), f32),
        ],
        cost=cost(20 * n_sec * n_tok * half * span, 2 * n_tok * half * span),
        name="moments",
    )(*messages, *tables)
    other = swap(give, "section", 1)
    ready = shape((BLOCK + EXTRA_ROWS, width), bf16)
    pieces = call(
        functools.partial(centre_kernel, groups), [ready] * groups, 2, name="centre"
    )(keep, other)
    pieces = [pieces[0]] + [swap(pieces[k], "section", CORES * k) for k in range(1, groups)]
    joined = call(
        functools.partial(join_kernel, groups),
        shape((BLOCK + EXTRA_ROWS, groups * width), bf16),
        groups,
        name="join",
    )(*pieces)
    gathered = gather_tok(joined, n_tok)
    cov, mean = call(
        functools.partial(spread_kernel, n_tok),
        [shape((1, BLOCK, depth), f32), shape((1, depth), f32)],
        n_tok,
        name="spread",
    )(*gathered)
    return cov, mean


def gather_tok(own, n_tok):
    pieces = [None] * n_tok
    pieces[0] = own
    for k in range(2, n_tok, 2):
        pieces[k] = swap(own, "tok", k)
    for k in range(0, n_tok, 2):
        pieces[k + 1] = swap(pieces[k], "tok", 1)
    return pieces


def power_of_two(n):
    return n > 0 and n & (n - 1) == 0


def body(*args):
    n_sec, n_tok = lax.axis_size("section"), lax.axis_size("tok")
    rows, depth = args[0].shape
    lanes_whole = depth % (n_tok * max(n_sec // CORES, 1) * LANES) == 0
    if (
        lanes_whole
        and power_of_two(n_sec)
        and power_of_two(n_tok)
        and n_sec >= CORES
        and n_tok >= 2
        and rows % (CORES * 16) == 0
        and (2 * n_sec + 1) * PARTS <= LANES
    ):
        return sharded_body(*args)
    return pipelined_body(*args)


def solution(mesh):
    in_specs = (
        P("tok", None),
        P("tok"),
        P(),
        P("tok"),
        P("section", None),
        P("section", None),
        P("section", None),
        P("section", None),
        P("section", None),
        P("section"),
    )
    out_specs = (P("section", None, None), P("section", None))
    return jax.shard_map(body, mesh=mesh, in_specs=in_specs, out_specs=out_specs, check_vma=False)
```

```python
import functools

import jax
import jax.numpy as jnp
from jax import lax
from jax.experimental import pallas as pl
from jax.experimental.pallas import tpu as pltpu
from jax.sharding import PartitionSpec as P


LANES = 128
CORES = 2
PARTS = 3
PARAM_ROWS = 4
EXTRA_ROWS = 8
EPS = 1e-06
GELU_A = 0.7978845608028654
GELU_B = 0.044715 * GELU_A
VMEM = pl.BlockSpec(memory_space=pltpu.VMEM)
SMEM = pl.BlockSpec(memory_space=pltpu.SMEM)

BLOCK = 128
MICRO = 4


def from_behind(block, axis, distance):
    devices = range(lax.axis_size(axis))
    route = [(i - distance, i) for i in devices if i - distance in devices]
    return lax.ppermute(block, axis, route)


def layer_norm(values, gain, bias_row):
    centre = jnp.mean(values, axis=-1, keepdims=True)
    spread = jnp.mean(jnp.square(values - centre), axis=-1, keepdims=True)
    return (values - centre) * lax.rsqrt(spread + 1e-06) * gain + bias_row


def smoothing(act_row, weight_row, alpha_code):
    exponent = alpha_code.astype(jnp.float32) / 8.0
    return jnp.exp(exponent * jnp.log(act_row) + (exponent - 1.0) * jnp.log(weight_row))


def about_mean(sum_second, sum_first, own_count, mean_row):
    cross = (
        sum_first[:BLOCK][:, None] * mean_row[None, :]
        + mean_row[:BLOCK][:, None] * sum_first[None, :]
    )
    return sum_second - cross + own_count * (mean_row[:BLOCK][:, None] * mean_row[None, :])


def pipelined_body(
    patches,
    patch_ids,
    pos_table,
    token_counts,
    norm_gain,
    norm_bias,
    branch_scale,
    act_range,
    weight_range,
    alpha_index,
):
    sections = lax.axis_size("section")
    section_index = lax.axis_index("section")
    rows_here = patches.shape[0]
    width = patches.shape[1]
    micro_rows = rows_here // MICRO
    looked_up = jnp.take(pos_table, patch_ids, axis=0).astype(jnp.float32)
    start_rows = (patches.astype(jnp.float32) + looked_up).astype(jnp.bfloat16)
    positions = jnp.arange(rows_here, dtype=jnp.int32)
    valid_flat = (positions < token_counts[0]).astype(jnp.float32)
    factor = smoothing(act_range[0], weight_range[0], alpha_index[0])
    blocks = start_rows.reshape(MICRO, micro_rows, width)
    valid_rows = valid_flat.reshape(MICRO, micro_rows)

    def tick_step(tick, carry):
        incoming, stash = carry
        micro_index = tick - section_index
        active = jnp.logical_and(micro_index >= 0, micro_index < MICRO)
        safe_index = jnp.clip(micro_index, 0, MICRO - 1)
        own_block = lax.dynamic_index_in_dim(blocks, safe_index, 0, keepdims=False)
        current = jnp.where(section_index == 0, own_block, incoming)
        normed = layer_norm(current.astype(jnp.float32), norm_gain[0], norm_bias[0])
        smoothed = (normed / factor).astype(jnp.bfloat16)
        weight_mask = lax.dynamic_index_in_dim(valid_rows, safe_index, 0, keepdims=False).astype(
            jnp.bfloat16
        )
        masked = smoothed * weight_mask[:, None]
        previous = lax.dynamic_index_in_dim(stash, safe_index, 0, keepdims=False)
        kept = jnp.where(active, masked, previous)
        stash = lax.dynamic_update_index_in_dim(stash, kept, safe_index, 0)
        updated = (current.astype(jnp.float32) + branch_scale[0] * jax.nn.gelu(normed)).astype(
            jnp.bfloat16
        )
        passed = from_behind(updated, "section", 1)
        return (passed, stash)

    initial = (
        jnp.zeros((micro_rows, width), jnp.bfloat16),
        jnp.zeros((MICRO, micro_rows, width), jnp.bfloat16),
    )
    carried = lax.fori_loop(0, sections + MICRO - 1, tick_step, initial)
    masked = carried[1].reshape(rows_here, width)
    ones_row = jnp.ones((1, rows_here), jnp.bfloat16)
    sum_first = jnp.dot(ones_row, masked, preferred_element_type=jnp.float32)[0]
    sum_second = lax.dot_general(
        masked[:, :BLOCK], masked, (((0,), (0,)), ((), ())), preferred_element_type=jnp.float32
    )
    own_count = token_counts.astype(jnp.float32)
    total_count, channel_sums = lax.psum((own_count, sum_first), "tok")
    mean_row = channel_sums / total_count
    gram_block = lax.psum(about_mean(sum_second, sum_first, own_count, mean_row), "tok")
    return ((gram_block / total_count)[None], mean_row[None])


def swap(block, axis, mask):
    route = [(i, i ^ mask) for i in range(lax.axis_size(axis))]
    return lax.ppermute(block, axis, route)


def split_parts(value):
    parts = []
    for _ in range(PARTS):
        part = value.astype(jnp.bfloat16).astype(jnp.float32)
        parts.append(part)
        value = value - part
    return parts


def gelu_update(x, normed, scale):
    inner = normed * (GELU_A + GELU_B * (normed * normed))
    return x + (0.5 * scale) * (normed * (1.0 + jnp.tanh(inner)))


def params_kernel(gain, bias, scale, act, weight, alpha, out):
    exponent = alpha[0].astype(jnp.float32) / 8.0
    out[0:1, :] = gain[...]
    out[1:2, :] = bias[...]
    out[2:3, :] = scale[...]
    out[3:4, :] = jnp.exp((1.0 - exponent) * jnp.log(weight[...]) - exponent * jnp.log(act[...]))


def embed_kernel(patches, ids, table, out):
    rows, half = patches.shape[0], out.shape[0]
    core = lax.rem(lax.axis_index("section"), CORES)
    positions = table.shape[0]
    hits = lax.broadcasted_iota(jnp.int32, (positions, rows), 0) == ids[...]
    onehot = jnp.transpose(hits.astype(jnp.float32))
    mine = pl.ds(pl.multiple_of(core * half, half), half)
    picked = jnp.where(core == 0, onehot[0:half, :], onehot[half:rows, :]).astype(jnp.bfloat16)
    step = 2 * LANES
    for c in range(out.shape[1] // step):
        cols = slice(c * step, (c + 1) * step)
        looked_up = jnp.dot(picked, table[:, cols], preferred_element_type=jnp.float32)
        out[:, cols] = (patches[mine, cols].astype(jnp.float32) + looked_up).astype(jnp.bfloat16)


def stats_kernel(n_sec, n_tok, width, rb, *refs):
    hid, counts = refs[0], refs[1]
    tables = refs[2 : 2 + n_sec]
    outs = refs[2 + n_sec : 2 + n_sec + n_tok]
    par, state, tile = refs[2 + n_sec + n_tok :]
    half, depth = hid.shape
    columns = depth // LANES
    sec, tok = lax.axis_index("section"), lax.axis_index("tok")
    core, group = lax.rem(sec, CORES), lax.div(sec, CORES)
    groups = n_sec // CORES
    for k in range(n_sec):
        par[jnp.bitwise_xor(sec, k)] = tables[k][...]
    lane = lax.broadcasted_iota(jnp.int32, (rb, LANES), 1)

    def total(terms):
        acc = [None] * 4
        for i, term in enumerate(terms):
            acc[i % 4] = term if acc[i % 4] is None else acc[i % 4] + term
        return jnp.sum((acc[0] + acc[1]) + (acc[2] + acc[3]), axis=-1, keepdims=True)

    def col(c):
        return slice(c * LANES, (c + 1) * LANES)

    def measure_rows(layer):
        mu = total(state[:, col(c)].astype(jnp.float32) for c in range(columns)) * (1.0 / depth)
        var = total(
            jnp.square(state[:, col(c)].astype(jnp.float32) - mu) for c in range(columns)
        ) * (1.0 / depth)
        rstd = lax.rsqrt(var + EPS)
        found = tile[...]
        for v, value in enumerate((mu, rstd)):
            for p, part in enumerate(split_parts(value)):
                found = jnp.where(lane == (2 * layer + v) * PARTS + p, part, found)
        tile[...] = found
        return mu, rstd

    @pl.loop(0, half // rb)
    def _(block):
        rows = pl.ds(pl.multiple_of(block * rb, rb), rb)
        row_id = lax.broadcasted_iota(jnp.int32, (rb, LANES), 0) + core * half + block * rb
        valid = (row_id < counts[0]).astype(jnp.float32)
        tile[...] = jnp.where(lane == 2 * n_sec * PARTS, valid, 0.0)
        state[...] = hid[rows, :]

        @pl.loop(0, n_sec - 1)
        def _(layer):
            mu, rstd = measure_rows(layer)
            for c in range(columns):
                x = state[:, col(c)].astype(jnp.float32)
                normed = (x - mu) * rstd * par[layer, 0:1, col(c)] + par[layer, 1:2, col(c)]
                state[:, col(c)] = gelu_update(x, normed, par[layer, 2:3, col(c)]).astype(
                    jnp.bfloat16
                )

        measure_rows(n_sec - 1)
        packed = tile[...].astype(jnp.bfloat16)
        for k in range(n_tok):
            peer = jnp.bitwise_xor(tok, k)
            first = pl.multiple_of((peer * groups + group) * width, LANES)
            outs[k][rows, 0:width] = hid[rows, pl.ds(first, width)]
            outs[k][rows, width : width + BLOCK] = hid[rows, 0:BLOCK]
            outs[k][rows, width + BLOCK : width + BLOCK + LANES] = packed


def moments_kernel(n_sec, n_tok, width, *refs):
    messages = refs[:n_tok]
    tables = refs[n_tok : n_tok + n_sec]
    keep, give = refs[n_tok + n_sec : n_tok + n_sec + 2]
    par, msg, sel, dec, smoothed, count = refs[n_tok + n_sec + 2 :]
    half = messages[0].shape[0]
    span = width + BLOCK
    blocks = 2 * n_sec + 1
    sec, tok = lax.axis_index("section"), lax.axis_index("tok")
    core, group = lax.rem(sec, CORES), lax.div(sec, CORES)
    groups = n_sec // CORES
    first = pl.multiple_of((tok * groups + group) * width, LANES)
    for k in range(n_sec):
        layer = jnp.bitwise_xor(sec, k)
        par[layer, :, 0:width] = tables[k][:, pl.ds(first, width)]
        par[layer, :, width:span] = tables[k][:, 0:BLOCK]
    for k in range(n_tok):
        msg[k] = messages[k][...]
    for q in range(blocks):
        row = lax.broadcasted_iota(jnp.int32, (LANES, LANES), 0)
        hit = jnp.logical_and(row >= q * PARTS, row < (q + 1) * PARTS)
        sel[:, q * LANES : (q + 1) * LANES] = hit.astype(jnp.float32).astype(jnp.bfloat16)
    count[...] = jnp.zeros_like(count)

    @pl.loop(0, n_tok)
    def _(k):
        dec[...] = jnp.dot(
            msg[k, :, span : span + LANES], sel[...], preferred_element_type=jnp.float32
        )
        valid = dec[:, 2 * n_sec * LANES : (2 * n_sec + 1) * LANES]
        count[...] += jnp.sum(valid.reshape(half // 8, 8, LANES), axis=0)
        rows = pl.ds(pl.multiple_of(k * half, half), half)
        for c in range(span // LANES):
            cols = slice(c * LANES, (c + 1) * LANES)
            x = msg[k, :, cols].astype(jnp.float32)
            for layer in range(n_sec):
                mu = dec[:, 2 * layer * LANES : (2 * layer + 1) * LANES]
                rstd = dec[:, (2 * layer + 1) * LANES : (2 * layer + 2) * LANES]
                normed = (x - mu) * rstd * par[layer, 0:1, cols] + par[layer, 1:2, cols]
                smoothed[layer, rows, cols] = (normed * par[layer, 3:4, cols] * valid).astype(
                    jnp.bfloat16
                )
                if layer < n_sec - 1:
                    x = gelu_update(x, normed, par[layer, 2:3, cols])
                    x = x.astype(jnp.bfloat16).astype(jnp.float32)

    ones = jnp.ones((8, n_tok * half), jnp.bfloat16)
    used = jnp.sum(count[...], axis=0, keepdims=True)
    for target, parity in ((keep, core), (give, 1 - core)):
        for j in range(groups):
            layer = CORES * j + parity
            values = smoothed[layer]
            lead = values[:, width:span]
            target[j, 0:BLOCK, :] = lax.dot_general(
                lead,
                values[:, 0:width],
                (((0,), (0,)), ((), ())),
                preferred_element_type=jnp.float32,
            )
            sums = jnp.dot(ones, values, preferred_element_type=jnp.float32)
            target[j, BLOCK : BLOCK + EXTRA_ROWS, :] = jnp.zeros((EXTRA_ROWS, width), jnp.float32)
            target[j, BLOCK : BLOCK + 1, :] = sums[0:1, 0:width]
            target[j, BLOCK + 1 : BLOCK + 2, 0:BLOCK] = sums[0:1, width:span]
            target[j, BLOCK + 2 : BLOCK + 3, 0:LANES] = used


def centre_kernel(groups, keep, other, *outs):
    width = keep.shape[2]
    group = lax.div(lax.axis_index("section"), CORES)
    for k in range(groups):
        j = jnp.bitwise_xor(group, k)
        tail = keep[j, BLOCK : BLOCK + EXTRA_ROWS, :] + other[j, BLOCK : BLOCK + EXTRA_ROWS, :]
        inverse = 1.0 / tail[2:3, 0:LANES]
        lead = jnp.broadcast_to(tail[1:2, 0:BLOCK] * inverse, (BLOCK, BLOCK))
        lead = jnp.transpose(lead)
        row_id = lax.broadcasted_iota(jnp.int32, (EXTRA_ROWS, LANES), 0)
        for c in range(width // LANES):
            cols = slice(c * LANES, (c + 1) * LANES)
            mean = tail[0:1, cols] * inverse
            second = keep[j, 0:BLOCK, cols] + other[j, 0:BLOCK, cols]
            outs[k][0:BLOCK, cols] = (second * inverse - lead * mean).astype(jnp.bfloat16)
            extra = jnp.zeros((EXTRA_ROWS, LANES), jnp.float32)
            for p, part in enumerate(split_parts(mean)):
                extra = jnp.where(row_id == p, part, extra)
            outs[k][BLOCK : BLOCK + EXTRA_ROWS, cols] = extra.astype(jnp.bfloat16)


def column_of(groups, index, width):
    j, k = index
    tok = jnp.bitwise_xor(lax.axis_index("tok"), k)
    group = jnp.bitwise_xor(lax.div(lax.axis_index("section"), CORES), j)
    return pl.multiple_of((tok * groups + group) * width, LANES)


def spread(groups, indices, pieces, cov, stage, sems):
    width = stage.shape[2]
    copies = []
    for i, (index, piece) in enumerate(zip(indices, pieces)):
        stage[i] = piece[0:BLOCK, :].astype(jnp.float32)
        first = column_of(groups, index, width)
        copies.append(
            pltpu.make_async_copy(stage.at[i], cov.at[0, :, pl.ds(first, width)], sems.at[i])
        )
        copies[-1].start()
    return copies


def early_kernel(groups, indices, *refs):
    count = len(indices)
    cov, stage, sems = refs[count:]
    for copy in spread(groups, indices, refs[:count], cov, stage, sems):
        copy.wait()


def late_kernel(groups, indices, late, *refs):
    count = len(indices)
    pieces = refs[:count]
    _, cov, mean, stage, sems = refs[count:]
    copies = spread(groups, [indices[i] for i in late], [pieces[i] for i in late], cov, stage, sems)
    width = stage.shape[2]
    for index, piece in zip(indices, pieces):
        tail = piece[BLOCK : BLOCK + EXTRA_ROWS, :].astype(jnp.float32)
        row = tail[0:1, :]
        for p in range(1, PARTS):
            row = row + tail[p : p + 1, :]
        mean[0:1, pl.ds(column_of(groups, index, width), width)] = row
    for copy in copies:
        copy.wait()


def room(arrays, scratch=()):
    total = 0
    for item in list(arrays) + [x for x in scratch if hasattr(x, "inner_aval") or hasattr(x, "shape")]:
        size = jnp.dtype(item.dtype).itemsize
        dims = list(item.shape)
        for extent in dims[:-2]:
            size *= extent
        for extent, tile in zip(dims[-2:], (16, LANES) if len(dims) > 1 else (1,)):
            size *= -(-extent // tile) * tile
        total += size
    return total + (2 << 20)


def call(kernel, outs, args, scratch=(), smem=(), cost=None):
    sizes = [x for i, x in enumerate(args) if i not in smem] + jax.tree.leaves(outs)
    return pl.pallas_call(
        kernel,
        out_shape=outs,
        in_specs=[SMEM if i in smem else VMEM for i in range(len(args))],
        out_specs=jax.tree.map(lambda _: VMEM, outs),
        scratch_shapes=list(scratch),
        cost_estimate=cost,
        compiler_params=pltpu.CompilerParams(vmem_limit_bytes=room(sizes, scratch)),
    )(*args)


def cost(flops, moved, slow=0):
    return pl.CostEstimate(flops=flops, bytes_accessed=moved, transcendentals=slow)


def sharded_body(
    patches,
    patch_ids,
    pos_table,
    token_counts,
    norm_gain,
    norm_bias,
    branch_scale,
    act_range,
    weight_range,
    alpha_index,
):
    n_sec, n_tok = lax.axis_size("section"), lax.axis_size("tok")
    groups = n_sec // CORES
    rows, depth = patches.shape
    half = rows // CORES
    positions = pos_table.shape[0]
    width = depth // (n_tok * groups)
    span = width + BLOCK
    f32, bf16 = jnp.float32, jnp.bfloat16
    shape = jax.ShapeDtypeStruct

    own = call(
        params_kernel,
        shape((PARAM_ROWS, depth), f32),
        [norm_gain, norm_bias, branch_scale, act_range, weight_range, alpha_index],
        smem=(5,),
    )
    tables = [own] + [swap(own, "section", k) for k in range(1, n_sec)]

    hidden = call(
        embed_kernel,
        shape((half, depth), bf16),
        [patches, patch_ids.reshape(1, rows), pos_table],
        cost=cost(2 * half * positions * depth, 2 * depth * (rows + positions + half)),
    )

    rb = 32 if half % 32 == 0 else 16
    work = half * depth * n_sec
    message = shape((half, span + LANES), bf16)
    messages = call(
        functools.partial(stats_kernel, n_sec, n_tok, width, rb),
        [message] * n_tok,
        [hidden, token_counts, *tables],
        scratch=[
            pltpu.VMEM((n_sec, PARAM_ROWS, depth), f32),
            pltpu.VMEM((rb, depth), bf16),
            pltpu.VMEM((rb, LANES), f32),
        ],
        smem=(1,),
        cost=cost(20 * work, 2 * half * depth, work),
    )
    messages = [messages[0]] + [swap(messages[k], "tok", k) for k in range(1, n_tok)]

    partial = shape((groups, BLOCK + EXTRA_ROWS, width), f32)
    keep, give = call(
        functools.partial(moments_kernel, n_sec, n_tok, width),
        [partial, partial],
        [*messages, *tables],
        scratch=[
            pltpu.VMEM((n_sec, PARAM_ROWS, span), f32),
            pltpu.VMEM((n_tok, half, span + LANES), bf16),
            pltpu.VMEM((LANES, (2 * n_sec + 1) * LANES), bf16),
            pltpu.VMEM((half, (2 * n_sec + 1) * LANES), f32),
            pltpu.VMEM((n_sec, n_tok * half, span), bf16),
            pltpu.VMEM((8, LANES), f32),
        ],
        cost=cost(20 * n_sec * n_tok * half * span, 2 * n_tok * half * span),
    )
    other = swap(give, "section", 1)
    ready = shape((BLOCK + EXTRA_ROWS, width), bf16)
    pieces = call(functools.partial(centre_kernel, groups), [ready] * groups, [keep, other])
    pieces = [pieces[0]] + [swap(pieces[k], "section", CORES * k) for k in range(1, groups)]
    indices, gathered = [], []
    for j in range(groups):
        for k, piece in enumerate(gather_tok(pieces[j], n_tok)):
            indices.append((j, k))
            gathered.append(piece)
    last = groups - 1
    late = [i for i, (j, k) in enumerate(indices) if k == n_tok - 1 or j == last and k in LATE]
    early = [i for i in range(len(indices)) if i not in late]

    def staging(count):
        return [pltpu.VMEM((count, BLOCK, width), f32), pltpu.SemaphoreType.DMA((count,))]

    full = shape((1, BLOCK, depth), f32)
    moved = 6 * BLOCK * width
    cov = pl.pallas_call(
        functools.partial(early_kernel, groups, [indices[i] for i in early]),
        out_shape=full,
        in_specs=[VMEM] * len(early),
        out_specs=pl.BlockSpec(memory_space=pl.ANY),
        scratch_shapes=staging(len(early)),
        compiler_params=pltpu.CompilerParams(
            vmem_limit_bytes=room([ready] * len(early), staging(len(early))[:1])
        ),
        cost_estimate=cost(len(early) * BLOCK * width, len(early) * moved),
        name="early",
    )(*[gathered[i] for i in early])
    return pl.pallas_call(
        functools.partial(late_kernel, groups, indices, late),
        out_shape=[full, shape((1, depth), f32)],
        in_specs=[VMEM] * len(indices) + [pl.BlockSpec(memory_space=pl.ANY)],
        out_specs=[pl.BlockSpec(memory_space=pl.ANY), VMEM],
        scratch_shapes=staging(len(late)),
        input_output_aliases={len(indices): 0},
        compiler_params=pltpu.CompilerParams(
            vmem_limit_bytes=room([ready] * len(indices), staging(len(late))[:1])
        ),
        cost_estimate=cost(len(late) * BLOCK * width, len(late) * moved),
        name="late",
    )(*gathered, cov)


def gather_tok(own, n_tok):
    pieces = [own] + [None] * (n_tok - 1)
    for k in range(1, n_tok):
        if k == 1 or k & (k - 1) == 0:
            pieces[k] = swap(own, "tok", k)
        elif k & 1:
            pieces[k] = swap(pieces[k - 1], "tok", 1)
        else:
            low = k & -k
            pieces[k] = swap(pieces[k - low], "tok", low)
    return pieces


LATE = (3, 5)


def power_of_two(n):
    return n > 0 and n & (n - 1) == 0


def body(*args):
    n_sec, n_tok = lax.axis_size("section"), lax.axis_size("tok")
    rows, depth = args[0].shape
    lanes_whole = depth % (n_tok * max(n_sec // CORES, 1) * LANES) == 0
    if (
        lanes_whole
        and power_of_two(n_sec)
        and power_of_two(n_tok)
        and n_sec >= CORES
        and n_tok >= 2
        and rows % (CORES * 16) == 0
        and (2 * n_sec + 1) * PARTS <= LANES
    ):
        return sharded_body(*args)
    return pipelined_body(*args)


def solution(mesh):
    in_specs = (
        P("tok", None),
        P("tok"),
        P(),
        P("tok"),
        P("section", None),
        P("section", None),
        P("section", None),
        P("section", None),
        P("section", None),
        P("section"),
    )
    out_specs = (P("section", None, None), P("section", None))
    return jax.shard_map(body, mesh=mesh, in_specs=in_specs, out_specs=out_specs, check_vma=False)
```
